32 devices in a mesh: leaf: 8 (over y, x, core), seq: 4 (over z).
Axes of the slice: x: 2, y: 2, z: 4, core: 2. Of those that a mesh axis runs over, the one named last changes fastest.
Arguments:
- prompt_q: bfloat16 [8, 512, 1792], P('leaf', 'seq'), may hold values from -6 to 6
- prompt_k: bfloat16 [8, 512, 256], P('leaf', 'seq'), may hold values from -6 to 6
- prompt_value_rows: bfloat16 [8, 512, 256], P('leaf', 'seq'), may hold values from -6 to 6
- leaf_q: bfloat16 [8, 192, 1792], P('leaf', 'seq'), may hold values from -6 to 6
- leaf_k: bfloat16 [8, 192, 256], P('leaf', 'seq'), may hold values from -6 to 6
- leaf_value_rows: bfloat16 [8, 192, 256], P('leaf', 'seq'), may hold values from -6 to 6
- prompt_dy: bfloat16 [8, 512, 3584], P('leaf', 'seq'), may hold values from -6 to 6
- leaf_dy: bfloat16 [8, 192, 3584], P('leaf', 'seq'), may hold values from -6 to 6
- out_weight: bfloat16 [1792, 3584], replicated, may hold values from -0.125 to 0.125
- lengths: int32 [8, 16], P('leaf'), may hold values from 1 to 24, 192 in all within a row
- offsets: int32 [8, 16], P('leaf'), may hold values from 1 to 512
- parents: int32 [8, 16], P('leaf'), may hold values from 0 to 15, as said below
Outputs:
- prompt_dq: float32 [8, 512, 1792], P('leaf', 'seq')
- prompt_dk: float32 [8, 512, 256], P('leaf', 'seq')
- prompt_dv: float32 [8, 512, 256], P('leaf', 'seq')
- leaf_dq: float32 [8, 192, 1792], P('leaf', 'seq')
- leaf_dk: float32 [8, 192, 256], P('leaf', 'seq')
- leaf_dv: float32 [8, 192, 256], P('leaf', 'seq')
- weight_grad: float32 [1792, 3584], P(('leaf', 'seq'))
The draws below stay inside these ranges and needn't reach their ends.
Inputs may be any that keep to these rules, and one draw needn't show every extreme that they name: parents[t, b] lies in 0 to b; the value b means that branch b has no ancestor branch.
All inputs are finite; a program needn't handle non-finite values.
Results may differ from the reference program's by a relative error of at most 0.025.
Values may be sent and summed in bfloat16 or wider, within the bound.
No kernel may reach another device: no remote copies, remote signals or barrier semaphores. Data moves between devices by JAX's collectives and lax.ppermute only.
A program may use at most 128 MiB of HBM per device.

```python
import math
import jax
import jax.numpy as jnp
import numpy as np
from jax import lax

D = 3584
HEAD_SIZE = 128
QUERY_HEADS = 14
KEY_VALUE_HEADS = 2
QUERY_PER_KV = 7
BRANCHES = 16
SEARCH_TREES = 8
PROMPT_TOKENS = 512
LEAF_TOKENS = 192
MOSTLEN = 24


def simple_sample(key, shape):
    return jnp.clip(jax.random.normal(jax.random.fold_in(key, 6), shape), -4.0, 4.0)


def draw_prompt_q(key, part):
    sampled_values = simple_sample(jax.random.fold_in(key, 13), (SEARCH_TREES, PROMPT_TOKENS, QUERY_HEADS * HEAD_SIZE))
    return sampled_values.astype(jnp.bfloat16)


def draw_prompt_k(key, part):
    sampled_values = simple_sample(jax.random.fold_in(key, 12), (SEARCH_TREES, PROMPT_TOKENS, KEY_VALUE_HEADS * HEAD_SIZE))
    return sampled_values.astype(jnp.bfloat16)


def draw_leaf_q(key, part):
    sampled_values = simple_sample(jax.random.fold_in(key, 15), (SEARCH_TREES, LEAF_TOKENS, QUERY_HEADS * HEAD_SIZE))
    return sampled_values.astype(jnp.bfloat16)


def draw_leaf_k(key, part):
    sampled_values = simple_sample(jax.random.fold_in(key, 14), (SEARCH_TREES, LEAF_TOKENS, KEY_VALUE_HEADS * HEAD_SIZE))
    return sampled_values.astype(jnp.bfloat16)


def draw_parents(key, part):
    branch_ids = jnp.arange(BRANCHES, dtype=jnp.int32)
    raw_draw = jax.random.randint(jax.random.fold_in(key, 16), (SEARCH_TREES, BRANCHES), 0, 4 * BRANCHES, dtype=jnp.int32)
    return (raw_draw % (branch_ids[None, :] + 1)).astype(jnp.int32)


def place_ends(values, rng, smallest, high):
    longest = values.shape.index(max(values.shape))
    spots = []
    for shift in (0, 1):
        where = [jax.random.randint(jax.random.fold_in(rng, axis), (), 0, length) for axis, length in enumerate(values.shape)]
        where[longest] = (where[longest] + shift) % values.shape[longest]
        spots.append(tuple(where))
    return values.at[spots[0]].set(smallest).at[spots[1]].set(high)


def levels(key, shape, pieces, smallest, largest):
    factor_of = 1.0
    for dim, shards_of in pieces:
        heights = jax.random.uniform(jax.random.fold_in(jax.random.fold_in(key, 6), dim), (shards_of,), jnp.float32, smallest / len(pieces), largest / len(pieces))
        factor_of = factor_of * jnp.repeat(jnp.exp(heights), shape[dim] // shards_of).reshape((-1,) + (1,) * (len(shape) - 1 - dim))
    return factor_of


def split_up(count, total, bound, slope):
    weights = [(1 << 20) // math.isqrt(rank ** slope) + 1 for rank in range(2, count + 1)]
    surplus, given = total - bound - (count - 1), [1] * (count - 1)
    while surplus > 0:
        candidates = [i for i in range(count - 1) if given[i] < bound]
        whole, left = sum([weights[i] for i in candidates]), surplus
        for i in candidates:
            extra = min(bound - given[i], max(1, left * weights[i] // whole), surplus)
            given[i] = given[i] + extra
            surplus = surplus - extra
    return np.array([bound] + given)


def ragged_sizes(own_key, amount, total, reach, skew):
    if amount == 2:
        one = jax.random.randint(own_key, (), max(1, total - reach), min(reach, total - 1) + 1)
        return jnp.stack([one, total - one])
    sizes = jnp.asarray(split_up(amount, total, reach, skew), jnp.int32)
    couples = (amount - 1) // 2
    giver, sink = sizes[1:1 + 2 * couples:2], sizes[2:2 + 2 * couples:2]
    margin = jnp.minimum(giver - 1, reach - sink)
    passed = jax.random.randint(jax.random.fold_in(own_key, 1), (couples,), 0, 1 << 20) % (margin + 1)
    sizes = sizes.at[1:1 + 2 * couples:2].set(giver - passed).at[2:2 + 2 * couples:2].set(sink + passed)
    return sizes[jax.random.permutation(jax.random.fold_in(own_key, 2), amount)]


def normal_values(own_key, dims, width, bound, cuts=(), kind=jnp.bfloat16):
    values = width * jax.random.normal(own_key, dims, jnp.float32)
    if cuts:
        values = values * levels(own_key, dims, cuts, -0.22, 0.18)
    return jnp.clip(values, -bound, bound).astype(kind)


def setup_inputs(seed: int = 0) -> dict:
    keys = jax.random.split(jax.random.key(seed), 13)
    return {
        "prompt_q": draw_prompt_q(jax.random.fold_in(keys[12], 71), 0),
        "prompt_k": draw_prompt_k(jax.random.fold_in(keys[12], 71), 0),
        "prompt_value_rows": normal_values(keys[2], (SEARCH_TREES, PROMPT_TOKENS, KEY_VALUE_HEADS * HEAD_SIZE), 1.0, 6.0, ((0, 8), (1, 4))),
        "leaf_q": draw_leaf_q(jax.random.fold_in(keys[12], 71), 0),
        "leaf_k": draw_leaf_k(jax.random.fold_in(keys[12], 71), 0),
        "leaf_value_rows": normal_values(keys[5], (SEARCH_TREES, LEAF_TOKENS, KEY_VALUE_HEADS * HEAD_SIZE), 1.0, 6.0, ((0, 8), (1, 4))),
        "prompt_dy": normal_values(keys[6], (SEARCH_TREES, PROMPT_TOKENS, D), 1.0, 6.0, ((0, 8), (1, 4))),
        "leaf_dy": normal_values(keys[7], (SEARCH_TREES, LEAF_TOKENS, D), 1.0, 6.0, ((0, 8), (1, 4))),
        "out_weight": normal_values(keys[8], (QUERY_HEADS * HEAD_SIZE, D), (QUERY_HEADS * HEAD_SIZE) ** -0.5, 0.125),
        "lengths": jax.vmap(lambda own: ragged_sizes(own, BRANCHES, LEAF_TOKENS, MOSTLEN, 2))(jax.random.split(keys[9], SEARCH_TREES)).reshape((SEARCH_TREES, BRANCHES)).astype(jnp.int32),
        "offsets": place_ends(jax.random.randint(keys[10], (SEARCH_TREES, BRANCHES), 1, PROMPT_TOKENS + 1), jax.random.fold_in(keys[10], 1), 1, PROMPT_TOKENS).astype(jnp.int32),
        "parents": draw_parents(jax.random.fold_in(keys[12], 71), 0),
    }


def leaf_visibility(lengths, offsets, parents, query_index, prompt_total, leaf_total):
    branch_ends = jnp.cumsum(lengths).astype(jnp.int32)
    branch_ids = jnp.arange(lengths.shape[0], dtype=jnp.int32)
    leaf_index = jnp.arange(leaf_total, dtype=jnp.int32)
    key_branch = lax.optimization_barrier(jnp.sum((leaf_index[:, None] >= branch_ends[None, :]).astype(jnp.int32), axis=1))
    query_branch = lax.optimization_barrier(jnp.sum((query_index[:, None] >= branch_ends[None, :]).astype(jnp.int32), axis=1))
    member = (query_branch[:, None] == branch_ids[None, :]).astype(jnp.int32)
    fork_point = lax.optimization_barrier(jnp.sum(member * offsets[None, :], axis=1))
    ancestor = lax.optimization_barrier(jnp.sum(member * parents[None, :], axis=1))
    prompt_index = jnp.arange(prompt_total, dtype=jnp.int32)
    sees_prompt = prompt_index[None, :] < fork_point[:, None]
    own_branch = (key_branch[None, :] == query_branch[:, None]) & (leaf_index[None, :] <= query_index[:, None])
    inherited = (key_branch[None, :] == ancestor[:, None]) & (ancestor[:, None] != query_branch[:, None])
    return jnp.concatenate([sees_prompt, own_branch | inherited], axis=1)

def tree_pass(query_rows, key_rows, value_rows, upstream, out_weight, visible):
    count_of_rows = query_rows.shape[0]
    score_scale = 1.0 / math.sqrt(HEAD_SIZE)
    grouped_queries = query_rows.reshape(count_of_rows, KEY_VALUE_HEADS, QUERY_PER_KV, HEAD_SIZE).astype(jnp.float32)
    output_gradient = jnp.dot(upstream, out_weight.T, preferred_element_type=jnp.float32).astype(jnp.bfloat16)
    gradient_groups = output_gradient.reshape(count_of_rows, KEY_VALUE_HEADS, QUERY_PER_KV, HEAD_SIZE).astype(jnp.float32)
    attn_parts, dq_parts, dk_parts, dv_parts = ([], [], [], [])
    for key_value_group in range(KEY_VALUE_HEADS):
        key_block = key_rows[:, key_value_group * HEAD_SIZE:(key_value_group + 1) * HEAD_SIZE].astype(jnp.float32)
        value_block = value_rows[:, key_value_group * HEAD_SIZE:(key_value_group + 1) * HEAD_SIZE].astype(jnp.float32)
        scores = jnp.einsum('qhd,kd->hqk', grouped_queries[:, key_value_group], key_block) * score_scale
        scores = jnp.where(visible[None], scores, -jnp.inf)
        shifted = jnp.exp(scores - lax.optimization_barrier(jnp.max(scores, axis=2, keepdims=True)))
        probabilities = shifted / lax.optimization_barrier(jnp.sum(shifted, axis=2, keepdims=True))
        weights = probabilities.astype(jnp.bfloat16).astype(jnp.float32)
        attn_block = jnp.einsum('hqk,kd->qhd', weights, value_block).astype(jnp.bfloat16)
        row_dot = lax.optimization_barrier(jnp.sum(gradient_groups[:, key_value_group] * attn_block.astype(jnp.float32), axis=2))
        prob_grad = jnp.einsum('qhd,kd->hqk', gradient_groups[:, key_value_group], value_block)
        dscore = (probabilities * (prob_grad - row_dot.T[:, :, None]) * score_scale).astype(jnp.bfloat16).astype(jnp.float32)
        dq_parts.append(jnp.einsum('hqk,kd->qhd', dscore, key_block))
        dk_parts.append(jnp.einsum('hqk,qhd->kd', dscore, grouped_queries[:, key_value_group]))
        dv_parts.append(jnp.einsum('hqk,qhd->kd', weights, gradient_groups[:, key_value_group]))
        attn_parts.append(attn_block)
    attn_out = jnp.stack(attn_parts, axis=1).reshape(count_of_rows, QUERY_HEADS * HEAD_SIZE)
    query_grad = jnp.stack(dq_parts, axis=1).reshape(count_of_rows, QUERY_HEADS * HEAD_SIZE)
    return (attn_out, query_grad, jnp.concatenate(dk_parts, axis=1), jnp.concatenate(dv_parts, axis=1))

def reference(prompt_q, prompt_k, prompt_value_rows, leaf_q, leaf_k, leaf_value_rows, prompt_dy, leaf_dy, out_weight, lengths, offsets, parents):
    prompt_index = jnp.arange(PROMPT_TOKENS, dtype=jnp.int32)
    prompt_sees = jnp.concatenate([prompt_index[None, :] <= prompt_index[:, None], jnp.zeros((PROMPT_TOKENS, LEAF_TOKENS), dtype=jnp.bool_)], axis=1)
    leaf_index = jnp.arange(LEAF_TOKENS, dtype=jnp.int32)

    def one_tree(tree_index):
        query_rows = jnp.concatenate([prompt_q[tree_index], leaf_q[tree_index]], axis=0)
        key_rows = jnp.concatenate([prompt_k[tree_index], leaf_k[tree_index]], axis=0)
        value_rows = jnp.concatenate([prompt_value_rows[tree_index], leaf_value_rows[tree_index]], axis=0)
        upstream = jnp.concatenate([prompt_dy[tree_index], leaf_dy[tree_index]], axis=0)
        leaf_sees = leaf_visibility(lengths[tree_index], offsets[tree_index], parents[tree_index], leaf_index, PROMPT_TOKENS, LEAF_TOKENS)
        visible = jnp.concatenate([prompt_sees, leaf_sees], axis=0)
        return tree_pass(query_rows, key_rows, value_rows, upstream, out_weight, visible)
    attn_out, query_grad, key_grad, value_grad = lax.map(one_tree, jnp.arange(SEARCH_TREES, dtype=jnp.int32))
    upstream_all = jnp.concatenate([prompt_dy, leaf_dy], axis=1)
    summed = jnp.dot(attn_out.reshape(-1, QUERY_HEADS * HEAD_SIZE).T, upstream_all.reshape(-1, D), preferred_element_type=jnp.float32)
    weight_grad = summed * (1.0 / math.sqrt(SEARCH_TREES * (PROMPT_TOKENS + LEAF_TOKENS)))
    return (query_grad[:, :PROMPT_TOKENS], key_grad[:, :PROMPT_TOKENS], value_grad[:, :PROMPT_TOKENS], query_grad[:, PROMPT_TOKENS:], key_grad[:, PROMPT_TOKENS:], value_grad[:, PROMPT_TOKENS:], weight_grad)
```

```python
import functools
import math

import jax
import jax.numpy as jnp
from jax import lax
from jax.experimental import pallas as pl
from jax.experimental.pallas import tpu as pltpu
from jax.sharding import PartitionSpec as P

HEAD_SIZE = 128
QUERY_HEADS = 14
KEY_VALUE_HEADS = 2
QUERY_PER_KV = 7
CORES = 2
COLUMN_CHUNKS = 2
MASKED = -1e30
HIDDEN_KEY = 1 << 20


NT = (((1,), (1,)), ((), ()))
NN = (((1,), (0,)), ((), ()))
TN = (((0,), (0,)), ((), ()))


def matmul(a, b, dims):
    return lax.dot_general(a, b, dims, preferred_element_type=jnp.float32)


def visibility_bias(seq_ref, lengths_ref, offsets_ref, parents_ref, starts_ref, bias_ref, prompt_dev, leaf_dev, seq_count):
    device_rows = prompt_dev + leaf_dev
    total = device_rows * seq_count
    seq_index = seq_ref[0]
    column = lax.broadcasted_iota(jnp.int32, (1, total), 1)
    slot = jnp.zeros_like(column)
    for edge in range(1, seq_count):
        slot = slot + (column >= edge * device_rows).astype(jnp.int32)
    local = column - slot * device_rows
    owner = seq_index - slot
    owner = jnp.where(owner < 0, owner + seq_count, owner)
    is_prompt = local < prompt_dev
    key_prompt = jnp.where(is_prompt, owner * prompt_dev + local, HIDDEN_KEY)
    key_leaf = jnp.where(is_prompt, -1, owner * leaf_dev + local - prompt_dev)
    prompt_query = seq_index * prompt_dev + lax.broadcasted_iota(jnp.int32, (prompt_dev, 1), 0)
    bias_ref[:prompt_dev, :] = jnp.where(key_prompt <= prompt_query, 0.0, MASKED)
    leaf_query = seq_index * leaf_dev + lax.broadcasted_iota(jnp.int32, (leaf_dev, 1), 0)
    fork = jnp.zeros_like(leaf_query)
    own_start = jnp.zeros_like(leaf_query)
    ancestor_start = jnp.zeros_like(leaf_query)
    ancestor_end = jnp.zeros_like(leaf_query)
    start = jnp.int32(0)
    for branch in range(lengths_ref.shape[1]):
        starts_ref[branch] = start
        end = start + lengths_ref[0, branch]
        parent = parents_ref[0, branch]
        has_ancestor = parent != branch
        parent_start = starts_ref[parent]
        parent_end = parent_start + lengths_ref[0, parent]
        inside = (leaf_query >= start) & (leaf_query < end)
        fork = jnp.where(inside, offsets_ref[0, branch], fork)
        own_start = jnp.where(inside, start, own_start)
        ancestor_start = jnp.where(inside, jnp.where(has_ancestor, parent_start, 0), ancestor_start)
        ancestor_end = jnp.where(inside, jnp.where(has_ancestor, parent_end, 0), ancestor_end)
        start = end
    sees = (
        (key_prompt < fork)
        | ((key_leaf >= own_start) & (key_leaf <= leaf_query))
        | ((key_leaf >= ancestor_start) & (key_leaf < ancestor_end))
    )
    bias_ref[prompt_dev:, :] = jnp.where(sees, 0.0, MASKED)


def head_columns(head):
    return pl.ds(pl.multiple_of(head * HEAD_SIZE, HEAD_SIZE), HEAD_SIZE)


def forward_kernel(seq_count, seq_ref, lengths_ref, offsets_ref, parents_ref, prompt_q_ref, leaf_q_ref, *rest):
    slots = rest[:seq_count]
    attn_ref, stat_ref, key_ref, value_ref, bias_ref, query_ref, starts_ref = rest[seq_count:]
    prompt_dev, leaf_dev = prompt_q_ref.shape[0], leaf_q_ref.shape[0]
    device_rows = prompt_dev + leaf_dev
    width = KEY_VALUE_HEADS * HEAD_SIZE
    visibility_bias(seq_ref, lengths_ref, offsets_ref, parents_ref, starts_ref, bias_ref, prompt_dev, leaf_dev, seq_count)
    query_ref[:prompt_dev, :] = prompt_q_ref[...]
    query_ref[prompt_dev:, :] = leaf_q_ref[...]
    for k in range(seq_count):
        rows = pl.ds(k * device_rows, device_rows)
        key_ref[rows, :] = slots[k][:, :width]
        value_ref[rows, :] = slots[k][:, width:]
    scale = 1.0 / math.sqrt(HEAD_SIZE)

    def step(member, carry):
        for group in range(KEY_VALUE_HEADS):
            head = group * QUERY_PER_KV + member
            cols = head_columns(head)
            group_cols = slice(group * HEAD_SIZE, (group + 1) * HEAD_SIZE)
            scores = matmul(query_ref[:, cols], key_ref[:, group_cols], NT) * scale + bias_ref[...]
            top = jnp.max(scores, axis=1, keepdims=True)
            shifted = jnp.exp(scores - top)
            total = jnp.sum(shifted, axis=1, keepdims=True)
            weights = (shifted * (1.0 / total)).astype(jnp.bfloat16)
            attn_ref[:, cols] = matmul(weights, value_ref[:, group_cols], NN).astype(jnp.bfloat16)
            stat_ref[head] = top + jnp.log(total)
        return carry

    lax.fori_loop(0, QUERY_PER_KV, step, 0)


def backward_kernel(seq_count, seq_ref, lengths_ref, offsets_ref, parents_ref, prompt_q_ref, leaf_q_ref, grad_ref, attn_ref, stat_ref, *rest):
    slots = rest[:seq_count]
    prompt_dq_ref, leaf_dq_ref = rest[seq_count:seq_count + 2]
    part_refs = rest[seq_count + 2:2 * seq_count + 2]
    key_ref, value_ref, bias_ref, query_ref, key_grad_ref, value_grad_ref, starts_ref = rest[2 * seq_count + 2:]
    prompt_dev, leaf_dev = prompt_q_ref.shape[0], leaf_q_ref.shape[0]
    device_rows = prompt_dev + leaf_dev
    width = KEY_VALUE_HEADS * HEAD_SIZE
    visibility_bias(seq_ref, lengths_ref, offsets_ref, parents_ref, starts_ref, bias_ref, prompt_dev, leaf_dev, seq_count)
    query_ref[:prompt_dev, :] = prompt_q_ref[...]
    query_ref[prompt_dev:, :] = leaf_q_ref[...]
    for k in range(seq_count):
        rows = pl.ds(k * device_rows, device_rows)
        key_ref[rows, :] = slots[k][:, :width]
        value_ref[rows, :] = slots[k][:, width:]
    key_grad_ref[...] = jnp.zeros_like(key_grad_ref)
    value_grad_ref[...] = jnp.zeros_like(value_grad_ref)
    scale = 1.0 / math.sqrt(HEAD_SIZE)

    def step(member, carry):
        for group in range(KEY_VALUE_HEADS):
            head = group * QUERY_PER_KV + member
            cols = head_columns(head)
            group_cols = slice(group * HEAD_SIZE, (group + 1) * HEAD_SIZE)
            query = query_ref[:, cols]
            grad = grad_ref[:, cols]
            keys = key_ref[:, group_cols]
            values = value_ref[:, group_cols]
            scores = matmul(query, keys, NT) * scale + bias_ref[...]
            probs = jnp.exp(scores - stat_ref[head])
            row_dot = jnp.sum(grad.astype(jnp.float32) * attn_ref[:, cols].astype(jnp.float32), axis=1, keepdims=True)
            dscore = (probs * ((matmul(grad, values, NT) - row_dot) * scale)).astype(jnp.bfloat16)
            query_grad = matmul(dscore, keys, NN)
            prompt_dq_ref[:, cols] = query_grad[:prompt_dev]
            leaf_dq_ref[:, cols] = query_grad[prompt_dev:]
            key_grad_ref[:, group_cols] += matmul(dscore, query, TN)
            value_grad_ref[:, group_cols] += matmul(probs.astype(jnp.bfloat16), grad, TN)
        return carry

    lax.fori_loop(0, QUERY_PER_KV, step, 0)
    for k in range(seq_count):
        rows = pl.ds(k * device_rows, device_rows)
        part_refs[k][:, :width] = key_grad_ref[rows, :].astype(part_refs[k].dtype)
        part_refs[k][:, width:] = value_grad_ref[rows, :].astype(part_refs[k].dtype)


def vmem():
    return pl.BlockSpec(memory_space=pltpu.VMEM)


def smem():
    return pl.BlockSpec(memory_space=pltpu.SMEM)


def grad_kernel(prompt_dy_ref, leaf_dy_ref, weight_ref, out_ref):
    prompt_dev = prompt_dy_ref.shape[0]
    weight = weight_ref[...]
    out_ref[:prompt_dev, :] = matmul(prompt_dy_ref[...], weight, NT).astype(jnp.bfloat16)
    out_ref[prompt_dev:, :] = matmul(leaf_dy_ref[...], weight, NT).astype(jnp.bfloat16)


def output_gradient(prompt_dy, leaf_dy, out_weight):
    prompt_dev, leaf_dev = prompt_dy.shape[0], leaf_dy.shape[0]
    rows = prompt_dev + leaf_dev
    width, model = out_weight.shape
    block = 2 * HEAD_SIZE
    return pl.pallas_call(
        grad_kernel,
        out_shape=jax.ShapeDtypeStruct((rows, width), jnp.bfloat16),
        grid=(width // block,),
        in_specs=[
            pl.BlockSpec((prompt_dev, model), lambda i: (0, 0)),
            pl.BlockSpec((leaf_dev, model), lambda i: (0, 0)),
            pl.BlockSpec((block, model), lambda i: (i, 0)),
        ],
        out_specs=pl.BlockSpec((rows, block), lambda i: (0, i)),
        cost_estimate=pl.CostEstimate(flops=2 * rows * width * model, bytes_accessed=2 * width * model, transcendentals=0),
    )(prompt_dy, leaf_dy, out_weight)


def outer_kernel(count, chip_rows, seq_ref, *refs):
    lefts, rights = refs[:count], refs[count:2 * count]
    outs, total_ref = refs[2 * count:-1], refs[-1]
    seq_count = len(outs)
    total = matmul(lefts[0][...], rights[0][...], TN)
    for left, right in zip(lefts[1:], rights[1:]):
        total = total + matmul(left[...], right[...], TN)
    total_ref[...] = total
    share = chip_rows // (CORES * seq_count)
    seq_index = seq_ref[0]
    for k in range(seq_count):
        target = lax.rem(seq_index + k, seq_count)
        for core in range(CORES):
            rows = pl.ds(pl.multiple_of((core * seq_count + target) * share, 8), share)
            outs[k][core * share:(core + 1) * share, :] = total_ref[rows, :].astype(outs[k].dtype)


def weight_partials(seq_index, lefts, rights, seq_count):
    chip_rows, columns = lefts[0].shape[1], rights[0].shape[1]
    share = chip_rows // (CORES * seq_count)
    if share % 8:
        total = matmul(jnp.concatenate(lefts, axis=0), jnp.concatenate(rights, axis=0), TN)
        total = total.reshape(CORES, seq_count, share, columns)
        parts = []
        for k in range(seq_count):
            picked = lax.dynamic_index_in_dim(total, (seq_index + k) % seq_count, 1, keepdims=False)
            parts.append(picked.reshape(CORES * share, columns).astype(jnp.bfloat16 if k else jnp.float32))
        return parts
    count = len(lefts)
    contraction = sum(left.shape[0] for left in lefts)
    return pl.pallas_call(
        functools.partial(outer_kernel, count, chip_rows),
        out_shape=[
            jax.ShapeDtypeStruct((CORES * share, columns), jnp.bfloat16 if k else jnp.float32) for k in range(seq_count)
        ],
        in_specs=[smem()] + [vmem()] * (2 * count),
        out_specs=[vmem()] * seq_count,
        scratch_shapes=[pltpu.VMEM((chip_rows, columns), jnp.float32)],
        cost_estimate=pl.CostEstimate(
            flops=2 * contraction * chip_rows * columns, bytes_accessed=2 * contraction * (chip_rows + columns), transcendentals=0
        ),
    )(seq_index.reshape(1), *lefts, *rights)


def xor_permute(array, axis, mask):
    count = lax.axis_size(axis)
    return lax.ppermute(array, axis, [(i, i ^ mask) for i in range(count)])


def shift_permute(array, axis, shift):
    count = lax.axis_size(axis)
    return lax.ppermute(array, axis, [(i, (i + shift) % count) for i in range(count)])


def gather_chips(own, partner, chip_count):
    if chip_count == 4:
        own_1 = xor_permute(own, "leaf", 1 * CORES)
        own_2 = xor_permute(own, "leaf", 2 * CORES)
        partner_2 = xor_permute(partner, "leaf", 2 * CORES)
        partner_1 = xor_permute(partner, "leaf", 1 * CORES)
        own_3 = xor_permute(own_1, "leaf", 2 * CORES)
        partner_3 = xor_permute(partner_2, "leaf", 1 * CORES)
        return [own, own_1, own_2, own_3, partner, partner_1, partner_2, partner_3]
    owns = [own] + [xor_permute(own, "leaf", k * CORES) for k in range(1, chip_count)]
    partners = [partner] + [xor_permute(partner, "leaf", k * CORES) for k in range(1, chip_count)]
    return owns + partners


def body(
    prompt_q,
    prompt_k,
    prompt_value_rows,
    leaf_q,
    leaf_k,
    leaf_value_rows,
    prompt_dy,
    leaf_dy,
    out_weight,
    lengths,
    offsets,
    parents,
):
    seq_count = lax.axis_size("seq")
    leaf_count = lax.axis_size("leaf")
    chip_count = leaf_count // CORES
    seq_index = lax.axis_index("seq").astype(jnp.int32)
    leaf_index = lax.axis_index("leaf")
    core = leaf_index % CORES
    chip = leaf_index // CORES
    prompt_dev, leaf_dev = prompt_q.shape[1], leaf_q.shape[1]
    device_rows = prompt_dev + leaf_dev
    width = KEY_VALUE_HEADS * HEAD_SIZE
    total_keys = device_rows * seq_count
    heads_width = QUERY_HEADS * HEAD_SIZE
    model = prompt_dy.shape[2]
    half = model // CORES
    chunk = half // COLUMN_CHUNKS
    normalizer = 1.0 / math.sqrt(leaf_count * seq_count * device_rows)

    key_values = jnp.concatenate(
        [
            jnp.concatenate([prompt_k[0], prompt_value_rows[0]], axis=1),
            jnp.concatenate([leaf_k[0], leaf_value_rows[0]], axis=1),
        ],
        axis=0,
    )
    slots = [key_values] + [shift_permute(key_values, "seq", k) for k in range(1, seq_count)]

    def column_piece(which, part):
        begin = which * half + part * chunk
        return jnp.concatenate([prompt_dy[0, :, begin:begin + chunk], leaf_dy[0, :, begin:begin + chunk]], axis=0)

    gathered = []
    for part in range(COLUMN_CHUNKS):
        first, second = column_piece(0, part), column_piece(1, part)
        kept = jnp.where(core == 0, first, second)
        given = jnp.where(core == 0, second, first)
        partner = xor_permute(given, "leaf", 1)
        gathered.append(gather_chips(kept, partner, chip_count))

    gradient = output_gradient(prompt_dy[0], leaf_dy[0], out_weight)
    seq_scalar = seq_index.reshape(1)
    pair_flops = 2 * QUERY_HEADS * device_rows * total_keys * HEAD_SIZE
    attn_out, stats = pl.pallas_call(
        functools.partial(forward_kernel, seq_count),
        out_shape=[
            jax.ShapeDtypeStruct((device_rows, heads_width), jnp.bfloat16),
            jax.ShapeDtypeStruct((QUERY_HEADS, device_rows, 1), jnp.float32),
        ],
        in_specs=[smem()] * 4 + [vmem()] * (2 + seq_count),
        out_specs=[vmem()] * 2,
        scratch_shapes=[
            pltpu.VMEM((total_keys, width), jnp.bfloat16),
            pltpu.VMEM((total_keys, width), jnp.bfloat16),
            pltpu.VMEM((device_rows, total_keys), jnp.float32),
            pltpu.VMEM((device_rows, heads_width), jnp.bfloat16),
            pltpu.SMEM((lengths.shape[1],), jnp.int32),
        ],
        cost_estimate=pl.CostEstimate(flops=2 * pair_flops, bytes_accessed=1 << 21, transcendentals=QUERY_HEADS * device_rows * total_keys),
    )(seq_scalar, lengths, offsets, parents, prompt_q[0], leaf_q[0], *slots)

    chip_rows = heads_width // chip_count
    blocks = attn_out.reshape(device_rows, chip_count, chip_rows)
    own_blocks = []
    for k in range(chip_count):
        block = lax.dynamic_index_in_dim(blocks, chip ^ k, 1, keepdims=False)
        own_blocks.append(xor_permute(block, "leaf", k * CORES) if k else block)
    lefts = own_blocks + [xor_permute(block, "leaf", 1) for block in own_blocks]

    backward = pl.pallas_call(
        functools.partial(backward_kernel, seq_count),
        out_shape=[
            jax.ShapeDtypeStruct((prompt_dev, heads_width), jnp.float32),
            jax.ShapeDtypeStruct((leaf_dev, heads_width), jnp.float32),
        ]
        + [jax.ShapeDtypeStruct((device_rows, 2 * width), jnp.bfloat16 if k else jnp.float32) for k in range(seq_count)],
        in_specs=[smem()] * 4 + [vmem()] * (5 + seq_count),
        out_specs=[vmem()] * (2 + seq_count),
        scratch_shapes=[
            pltpu.VMEM((total_keys, width), jnp.bfloat16),
            pltpu.VMEM((total_keys, width), jnp.bfloat16),
            pltpu.VMEM((device_rows, total_keys), jnp.float32),
            pltpu.VMEM((device_rows, heads_width), jnp.bfloat16),
            pltpu.VMEM((total_keys, width), jnp.float32),
            pltpu.VMEM((total_keys, width), jnp.float32),
            pltpu.SMEM((lengths.shape[1],), jnp.int32),
        ],
        cost_estimate=pl.CostEstimate(flops=5 * pair_flops, bytes_accessed=1 << 22, transcendentals=QUERY_HEADS * device_rows * total_keys),
    )(seq_scalar, lengths, offsets, parents, prompt_q[0], leaf_q[0], gradient, attn_out, stats, *slots)
    prompt_dq, leaf_dq = backward[:2]
    key_parts = backward[2:]
    key_grads = key_parts[0]
    for k in range(1, seq_count):
        key_grads = key_grads + shift_permute(key_parts[k], "seq", seq_count - k).astype(jnp.float32)

    share = chip_rows // (CORES * seq_count)
    mine, others = [], []
    for part in range(COLUMN_CHUNKS):
        parts = weight_partials(seq_index, lefts, gathered[part], seq_count)
        summed = parts[0]
        for k in range(1, seq_count):
            summed = summed + shift_permute(parts[k], "seq", k).astype(jnp.float32)
        summed = summed * normalizer
        keep = jnp.where(core == 0, summed[:share], summed[share:])
        give = jnp.where(core == 0, summed[share:], summed[:share])
        mine.append(keep)
        others.append(xor_permute(give, "leaf", 1))
    mine = jnp.concatenate(mine, axis=1)
    others = jnp.concatenate(others, axis=1)
    weight_grad = jnp.concatenate(
        [jnp.where(core == 0, mine, others), jnp.where(core == 0, others, mine)], axis=1
    )
    return (
        prompt_dq[None],
        key_grads[:prompt_dev, :width][None],
        key_grads[:prompt_dev, width:][None],
        leaf_dq[None],
        key_grads[prompt_dev:, :width][None],
        key_grads[prompt_dev:, width:][None],
        weight_grad,
    )


def solution(mesh):
    tokens = P("leaf", "seq", None)
    return jax.shard_map(
        body,
        mesh=mesh,
        in_specs=(tokens,) * 8 + (P(),) + (P("leaf", None),) * 3,
        out_specs=(tokens,) * 6 + (P(("leaf", "seq"), None),),
        check_vma=False,
    )
```

```python
import functools
import math

import jax
import jax.numpy as jnp
from jax import lax
from jax.experimental import pallas as pl
from jax.experimental.pallas import tpu as pltpu
from jax.sharding import PartitionSpec as P


HEAD_SIZE = 128
QUERY_HEADS = 14
KEY_VALUE_HEADS = 2
QUERY_PER_KV = 7
CORES = 2
COLUMN_CHUNKS = 2
MASKED = -1e30
HIDDEN_KEY = 1 << 20
LOG2E = math.log2(math.e)
VMEM_LIMIT = 32 << 20


NT = (((1,), (1,)), ((), ()))
NN = (((1,), (0,)), ((), ()))
TN = (((0,), (0,)), ((), ()))


def matmul(a, b, dims):
    return lax.dot_general(a, b, dims, preferred_element_type=jnp.float32)


def visibility_bias(seq_ref, lengths_ref, offsets_ref, parents_ref, starts_ref, bias_ref, prompt_dev, leaf_dev, seq_count):
    device_rows = prompt_dev + leaf_dev
    total = device_rows * seq_count
    seq_index = seq_ref[0]
    column = lax.broadcasted_iota(jnp.int32, (1, total), 1)
    slot = jnp.zeros_like(column)
    for edge in range(1, seq_count):
        slot = slot + (column >= edge * device_rows).astype(jnp.int32)
    local = column - slot * device_rows
    owner = seq_index - slot
    owner = jnp.where(owner < 0, owner + seq_count, owner)
    is_prompt = local < prompt_dev
    key_prompt = jnp.where(is_prompt, owner * prompt_dev + local, HIDDEN_KEY)
    key_leaf = jnp.where(is_prompt, -1, owner * leaf_dev + local - prompt_dev)
    prompt_query = seq_index * prompt_dev + lax.broadcasted_iota(jnp.int32, (prompt_dev, 1), 0)
    bias_ref[:prompt_dev, :] = jnp.where(key_prompt <= prompt_query, 0.0, MASKED)
    leaf_query = seq_index * leaf_dev + lax.broadcasted_iota(jnp.int32, (leaf_dev, 1), 0)
    fork = jnp.zeros_like(leaf_query)
    own_start = jnp.zeros_like(leaf_query)
    ancestor_start = jnp.zeros_like(leaf_query)
    ancestor_end = jnp.zeros_like(leaf_query)
    start = jnp.int32(0)
    for branch in range(lengths_ref.shape[1]):
        starts_ref[branch] = start
        end = start + lengths_ref[0, branch]
        parent = parents_ref[0, branch]
        has_ancestor = parent != branch
        parent_start = starts_ref[parent]
        parent_end = parent_start + lengths_ref[0, parent]
        inside = (leaf_query >= start) & (leaf_query < end)
        fork = jnp.where(inside, offsets_ref[0, branch], fork)
        own_start = jnp.where(inside, start, own_start)
        ancestor_start = jnp.where(inside, jnp.where(has_ancestor, parent_start, 0), ancestor_start)
        ancestor_end = jnp.where(inside, jnp.where(has_ancestor, parent_end, 0), ancestor_end)
        start = end
    sees = (
        (key_prompt < fork)
        | ((key_leaf >= own_start) & (key_leaf <= leaf_query))
        | ((key_leaf >= ancestor_start) & (key_leaf < ancestor_end))
    )
    bias_ref[prompt_dev:, :] = jnp.where(sees, 0.0, MASKED)


def head_columns(head):
    return pl.ds(pl.multiple_of(head * HEAD_SIZE, HEAD_SIZE), HEAD_SIZE)


def load_rows(prompt_q_ref, leaf_q_ref, query_ref):
    prompt_dev = prompt_q_ref.shape[0]
    query_ref[:prompt_dev, :] = prompt_q_ref[...]
    query_ref[prompt_dev:, :] = leaf_q_ref[...]


def forward_kernel(
    seq_count, chip_count, seq_ref, chip_ref, lengths_ref, offsets_ref, parents_ref, prompt_q_ref, leaf_q_ref, *rest
):
    slots = rest[:seq_count]
    attn_ref, stat_ref = rest[seq_count:seq_count + 2]
    block_refs = rest[seq_count + 2:seq_count + 2 + chip_count]
    key_ref, value_ref, bias_ref, query_ref, pick_ref, starts_ref = rest[seq_count + 2 + chip_count:]
    prompt_dev, leaf_dev = prompt_q_ref.shape[0], leaf_q_ref.shape[0]
    device_rows = prompt_dev + leaf_dev
    width = KEY_VALUE_HEADS * HEAD_SIZE
    visibility_bias(seq_ref, lengths_ref, offsets_ref, parents_ref, starts_ref, bias_ref, prompt_dev, leaf_dev, seq_count)
    load_rows(prompt_q_ref, leaf_q_ref, query_ref)
    for k in range(seq_count):
        rows = pl.ds(k * device_rows, device_rows)
        key_ref[rows, :] = slots[k][:, :width]
        for group in range(KEY_VALUE_HEADS):
            begin = width + group * HEAD_SIZE
            value_ref[group, rows, :HEAD_SIZE] = slots[k][:, begin:begin + HEAD_SIZE]
            value_ref[group, rows, HEAD_SIZE:] = jnp.ones((device_rows, HEAD_SIZE), jnp.bfloat16)
    scale = LOG2E / math.sqrt(HEAD_SIZE)

    def step(member, carry):
        for group in range(KEY_VALUE_HEADS):
            head = group * QUERY_PER_KV + member
            cols = head_columns(head)
            group_cols = slice(group * HEAD_SIZE, (group + 1) * HEAD_SIZE)
            scores = matmul(query_ref[:, cols], key_ref[:, group_cols], NT) * scale + bias_ref[...]
            top = jnp.max(scores, axis=1, keepdims=True)
            shifted = jnp.exp2(scores - top).astype(jnp.bfloat16)
            both = matmul(shifted, value_ref[group], NN)
            total = both[:, HEAD_SIZE:]
            attn_ref[:, cols] = (both[:, :HEAD_SIZE] * (1.0 / total)).astype(jnp.bfloat16)
            stat_ref[head] = top + jnp.log2(total)
        return carry

    lax.fori_loop(0, QUERY_PER_KV, step, 0, unroll=QUERY_PER_KV)
    chip_rows = attn_ref.shape[1] // chip_count
    for k in range(chip_count):
        pick_ref[k] = attn_ref[:, k * chip_rows:(k + 1) * chip_rows]
    for k in range(chip_count):
        block_refs[k][...] = pick_ref[chip_ref[0] ^ k]


def backward_kernel(
    seq_count, seq_ref, lengths_ref, offsets_ref, parents_ref, prompt_q_ref, leaf_q_ref, grad_ref, attn_ref, stat_ref, *rest
):
    slots = rest[:seq_count]
    prompt_dq_ref, leaf_dq_ref = rest[seq_count:seq_count + 2]
    part_refs = rest[seq_count + 2:2 * seq_count + 2]
    key_ref, value_ref, bias_ref, query_ref, dscore_ref, weight_ref, heads_q_ref, heads_g_ref, starts_ref = rest[2 * seq_count + 2:]
    prompt_dev, leaf_dev = prompt_q_ref.shape[0], leaf_q_ref.shape[0]
    device_rows = prompt_dev + leaf_dev
    width = KEY_VALUE_HEADS * HEAD_SIZE
    total_keys = device_rows * seq_count
    visibility_bias(seq_ref, lengths_ref, offsets_ref, parents_ref, starts_ref, bias_ref, prompt_dev, leaf_dev, seq_count)
    load_rows(prompt_q_ref, leaf_q_ref, query_ref)
    for k in range(seq_count):
        rows = pl.ds(k * device_rows, device_rows)
        key_ref[rows, :] = slots[k][:, :width]
        value_ref[rows, :] = slots[k][:, width:]
    scale = 1.0 / math.sqrt(HEAD_SIZE)
    copies = -(-total_keys // HEAD_SIZE)

    for group in range(KEY_VALUE_HEADS):
        group_cols = slice(group * HEAD_SIZE, (group + 1) * HEAD_SIZE)
        value_cols = slice(width + group * HEAD_SIZE, width + (group + 1) * HEAD_SIZE)
        keys = key_ref[:, group_cols]
        values = value_ref[:, group_cols]

        def step(member, carry):
            head = group * QUERY_PER_KV + member
            cols = head_columns(head)
            query = query_ref[:, cols]
            grad = grad_ref[:, cols]
            stat = jnp.concatenate([stat_ref[head]] * copies, axis=1)[:, :total_keys]
            scores = matmul(query, keys, NT) * (scale * LOG2E) + bias_ref[...]
            probs = jnp.exp2(scores - stat)
            row_dot = jnp.sum(grad.astype(jnp.float32) * attn_ref[:, cols].astype(jnp.float32), axis=1, keepdims=True)
            dscore = (probs * (matmul(grad, values, NT) - row_dot)).astype(jnp.bfloat16)
            query_grad = matmul(dscore, keys, NN) * scale
            prompt_dq_ref[:, cols] = query_grad[:prompt_dev]
            leaf_dq_ref[:, cols] = query_grad[prompt_dev:]
            rows = pl.ds(pl.multiple_of(member * device_rows, 16), device_rows)
            dscore_ref[rows, :] = dscore
            weight_ref[rows, :] = probs.astype(jnp.bfloat16)
            heads_q_ref[rows, :] = query
            heads_g_ref[rows, :] = grad
            return carry

        lax.fori_loop(0, QUERY_PER_KV, step, 0, unroll=QUERY_PER_KV)
        key_grad = matmul(dscore_ref[...], heads_q_ref[...], TN) * scale
        value_grad = matmul(weight_ref[...], heads_g_ref[...], TN)
        for k in range(seq_count):
            rows = slice(k * device_rows, (k + 1) * device_rows)
            part_refs[k][:, group_cols] = key_grad[rows].astype(part_refs[k].dtype)
            part_refs[k][:, value_cols] = value_grad[rows].astype(part_refs[k].dtype)


def vmem():
    return pl.BlockSpec(memory_space=pltpu.VMEM)


def smem():
    return pl.BlockSpec(memory_space=pltpu.SMEM)


def params():
    return pltpu.CompilerParams(vmem_limit_bytes=VMEM_LIMIT)


def grad_kernel(prompt_dy_ref, leaf_dy_ref, weight_ref, out_ref, rows_ref):
    @pl.when(pl.program_id(0) == 0)
    def _():
        load_rows(prompt_dy_ref, leaf_dy_ref, rows_ref)

    out_ref[...] = matmul(rows_ref[...], weight_ref[...], NT).astype(jnp.bfloat16)


def output_gradient(prompt_dy, leaf_dy, out_weight):
    prompt_dev, leaf_dev = prompt_dy.shape[0], leaf_dy.shape[0]
    rows = prompt_dev + leaf_dev
    width, model = out_weight.shape
    block = 2 * HEAD_SIZE
    return pl.pallas_call(
        grad_kernel,
        out_shape=jax.ShapeDtypeStruct((rows, width), jnp.bfloat16),
        grid=(width // block,),
        in_specs=[
            pl.BlockSpec((prompt_dev, model), lambda i: (0, 0)),
            pl.BlockSpec((leaf_dev, model), lambda i: (0, 0)),
            pl.BlockSpec((block, model), lambda i: (i, 0)),
        ],
        out_specs=pl.BlockSpec((rows, block), lambda i: (0, i)),
        scratch_shapes=[pltpu.VMEM((rows, model), jnp.bfloat16)],
        compiler_params=params(),
        cost_estimate=pl.CostEstimate(flops=2 * rows * width * model, bytes_accessed=2 * width * model, transcendentals=0),
    )(prompt_dy, leaf_dy, out_weight)


def outer_kernel(count, chip_rows, seq_ref, *refs):
    lefts, rights = refs[:count], refs[count:2 * count]
    outs, (total_ref, left_ref, right_ref) = refs[2 * count:-3], refs[-3:]
    seq_count = len(outs)
    tokens = lefts[0].shape[0]
    for tree in range(count):
        rows = slice(tree * tokens, (tree + 1) * tokens)
        left_ref[rows, :] = lefts[tree][...]
        right_ref[rows, :] = rights[tree][...]
    total_ref[...] = matmul(left_ref[...], right_ref[...], TN)
    share = chip_rows // (CORES * seq_count)
    for k in range(seq_count):
        target = lax.rem(seq_ref[0] + k, seq_count)
        for core in range(CORES):
            rows = pl.ds(pl.multiple_of((core * seq_count + target) * share, 8), share)
            outs[k][core * share:(core + 1) * share, :] = total_ref[rows, :].astype(outs[k].dtype)


def weight_partials(seq_index, lefts, rights, seq_count):
    chip_rows, columns = lefts[0].shape[1], rights[0].shape[1]
    share = chip_rows // (CORES * seq_count)
    if share % 8:
        total = matmul(jnp.concatenate(lefts, axis=0), jnp.concatenate(rights, axis=0), TN)
        total = total.reshape(CORES, seq_count, share, columns)
        parts = []
        for k in range(seq_count):
            picked = lax.dynamic_index_in_dim(total, (seq_index + k) % seq_count, 1, keepdims=False)
            parts.append(picked.reshape(CORES * share, columns).astype(jnp.bfloat16 if k else jnp.float32))
        return parts
    count = len(lefts)
    contraction = sum(left.shape[0] for left in lefts)
    return pl.pallas_call(
        functools.partial(outer_kernel, count, chip_rows),
        out_shape=[
            jax.ShapeDtypeStruct((CORES * share, columns), jnp.bfloat16 if k else jnp.float32) for k in range(seq_count)
        ],
        in_specs=[smem()] + [vmem()] * (2 * count),
        out_specs=[vmem()] * seq_count,
        scratch_shapes=[
            pltpu.VMEM((chip_rows, columns), jnp.float32),
            pltpu.VMEM((contraction, chip_rows), jnp.bfloat16),
            pltpu.VMEM((contraction, columns), jnp.bfloat16),
        ],
        compiler_params=params(),
        cost_estimate=pl.CostEstimate(
            flops=2 * contraction * chip_rows * columns, bytes_accessed=2 * contraction * (chip_rows + columns), transcendentals=0
        ),
    )(seq_index.reshape(1), *lefts, *rights)


def xor_permute(array, axis, mask):
    count = lax.axis_size(axis)
    return lax.ppermute(array, axis, [(i, i ^ mask) for i in range(count)])


def shift_permute(array, axis, shift):
    count = lax.axis_size(axis)
    return lax.ppermute(array, axis, [(i, (i + shift) % count) for i in range(count)])


def gather_chips(own, partner, chip_count):
    if chip_count == 4:
        own_1 = xor_permute(own, "leaf", 1 * CORES)
        own_2 = xor_permute(own, "leaf", 2 * CORES)
        partner_2 = xor_permute(partner, "leaf", 2 * CORES)
        partner_1 = xor_permute(partner, "leaf", 1 * CORES)
        own_3 = xor_permute(own_1, "leaf", 2 * CORES)
        partner_3 = xor_permute(partner_2, "leaf", 1 * CORES)
        return [own, own_1, own_2, own_3, partner, partner_1, partner_2, partner_3]
    owns = [own] + [xor_permute(own, "leaf", k * CORES) for k in range(1, chip_count)]
    partners = [partner] + [xor_permute(partner, "leaf", k * CORES) for k in range(1, chip_count)]
    return owns + partners


def body(
    prompt_q,
    prompt_k,
    prompt_value_rows,
    leaf_q,
    leaf_k,
    leaf_value_rows,
    prompt_dy,
    leaf_dy,
    out_weight,
    lengths,
    offsets,
    parents,
):
    seq_count = lax.axis_size("seq")
    leaf_count = lax.axis_size("leaf")
    chip_count = leaf_count // CORES
    seq_index = lax.axis_index("seq").astype(jnp.int32)
    leaf_index = lax.axis_index("leaf").astype(jnp.int32)
    core = leaf_index & 1
    chip = leaf_index >> 1
    prompt_dev, leaf_dev = prompt_q.shape[1], leaf_q.shape[1]
    device_rows = prompt_dev + leaf_dev
    width = KEY_VALUE_HEADS * HEAD_SIZE
    total_keys = device_rows * seq_count
    heads_width = QUERY_HEADS * HEAD_SIZE
    chip_rows = heads_width // chip_count
    share = chip_rows // (CORES * seq_count)
    half = prompt_dy.shape[2] // CORES
    chunk = half // COLUMN_CHUNKS
    normalizer = 1.0 / math.sqrt(leaf_count * seq_count * device_rows)
    seq_scalar, chip_scalar = seq_index.reshape(1), chip.reshape(1)

    key_values = jnp.concatenate(
        [
            jnp.concatenate([prompt_k[0], prompt_value_rows[0]], axis=1),
            jnp.concatenate([leaf_k[0], leaf_value_rows[0]], axis=1),
        ],
        axis=0,
    )
    slots = [key_values] + [shift_permute(key_values, "seq", k) for k in range(1, seq_count)]

    def column_piece(which, part):
        begin = which * half + part * chunk
        return jnp.concatenate([prompt_dy[0, :, begin:begin + chunk], leaf_dy[0, :, begin:begin + chunk]], axis=0)

    gathered = []
    for part in range(COLUMN_CHUNKS):
        first, second = column_piece(0, part), column_piece(1, part)
        kept = jnp.where(core == 0, first, second)
        given = jnp.where(core == 0, second, first)
        partner = xor_permute(given, "leaf", 1)
        gathered.append(gather_chips(kept, partner, chip_count))

    gradient = output_gradient(prompt_dy[0], leaf_dy[0], out_weight)
    pair_flops = 2 * QUERY_HEADS * device_rows * total_keys * HEAD_SIZE
    exps = QUERY_HEADS * device_rows * total_keys
    attention_scratch = [
        pltpu.VMEM((total_keys, width), jnp.bfloat16),
        pltpu.VMEM((total_keys, width), jnp.bfloat16),
        pltpu.VMEM((device_rows, total_keys), jnp.float32),
        pltpu.VMEM((device_rows, heads_width), jnp.bfloat16),
    ]
    branch_scratch = pltpu.SMEM((lengths.shape[1],), jnp.int32)
    forward = pl.pallas_call(
        functools.partial(forward_kernel, seq_count, chip_count),
        out_shape=[
            jax.ShapeDtypeStruct((device_rows, heads_width), jnp.bfloat16),
            jax.ShapeDtypeStruct((QUERY_HEADS, device_rows, HEAD_SIZE), jnp.float32),
        ]
        + [jax.ShapeDtypeStruct((device_rows, chip_rows), jnp.bfloat16)] * chip_count,
        in_specs=[smem()] * 5 + [vmem()] * (2 + seq_count),
        out_specs=[vmem()] * (2 + chip_count),
        scratch_shapes=[
            attention_scratch[0],
            pltpu.VMEM((KEY_VALUE_HEADS, total_keys, 2 * HEAD_SIZE), jnp.bfloat16),
            *attention_scratch[2:],
            pltpu.VMEM((chip_count, device_rows, chip_rows), jnp.bfloat16),
            branch_scratch,
        ],
        compiler_params=params(),
        cost_estimate=pl.CostEstimate(flops=2 * pair_flops, bytes_accessed=1 << 21, transcendentals=exps),
    )(seq_scalar, chip_scalar, lengths, offsets, parents, prompt_q[0], leaf_q[0], *slots)
    attn_out, stats = forward[:2]
    own_blocks = [forward[2]] + [xor_permute(forward[2 + k], "leaf", k * CORES) for k in range(1, chip_count)]
    lefts = own_blocks + [xor_permute(block, "leaf", 1) for block in own_blocks]

    backward = pl.pallas_call(
        functools.partial(backward_kernel, seq_count),
        out_shape=[
            jax.ShapeDtypeStruct((prompt_dev, heads_width), jnp.float32),
            jax.ShapeDtypeStruct((leaf_dev, heads_width), jnp.float32),
        ]
        + [jax.ShapeDtypeStruct((device_rows, 2 * width), jnp.bfloat16 if k else jnp.float32) for k in range(seq_count)],
        in_specs=[smem()] * 4 + [vmem()] * (5 + seq_count),
        out_specs=[vmem()] * (2 + seq_count),
        scratch_shapes=[
            *attention_scratch,
            pltpu.VMEM((QUERY_PER_KV * device_rows, total_keys), jnp.bfloat16),
            pltpu.VMEM((QUERY_PER_KV * device_rows, total_keys), jnp.bfloat16),
            pltpu.VMEM((QUERY_PER_KV * device_rows, HEAD_SIZE), jnp.bfloat16),
            pltpu.VMEM((QUERY_PER_KV * device_rows, HEAD_SIZE), jnp.bfloat16),
            branch_scratch,
        ],
        compiler_params=params(),
        cost_estimate=pl.CostEstimate(flops=5 * pair_flops, bytes_accessed=1 << 22, transcendentals=exps),
    )(seq_scalar, lengths, offsets, parents, prompt_q[0], leaf_q[0], gradient, attn_out, stats, *slots)
    prompt_dq, leaf_dq = backward[:2]
    key_parts = backward[2:]
    key_grads = key_parts[0]
    for k in range(1, seq_count):
        key_grads = key_grads + shift_permute(key_parts[k], "seq", seq_count - k).astype(jnp.float32)

    mine, others = [], []
    for part in range(COLUMN_CHUNKS):
        parts = weight_partials(seq_index, lefts, gathered[part], seq_count)
        summed = parts[0]
        for k in range(1, seq_count):
            summed = summed + shift_permute(parts[k], "seq", k).astype(jnp.float32)
        summed = summed * normalizer
        keep = jnp.where(core == 0, summed[:share], summed[share:])
        give = jnp.where(core == 0, summed[share:], summed[:share])
        mine.append(keep)
        others.append(xor_permute(give, "leaf", 1))
    mine = jnp.concatenate(mine, axis=1)
    others = jnp.concatenate(others, axis=1)
    weight_grad = jnp.concatenate(
        [jnp.where(core == 0, mine, others), jnp.where(core == 0, others, mine)], axis=1
    )
    return (
        prompt_dq[None],
        key_grads[:prompt_dev, :width][None],
        key_grads[:prompt_dev, width:][None],
        leaf_dq[None],
        key_grads[prompt_dev:, :width][None],
        key_grads[prompt_dev:, width:][None],
        weight_grad,
    )


def solution(mesh):
    tokens = P("leaf", "seq", None)
    return jax.shard_map(
        body,
        mesh=mesh,
        in_specs=(tokens,) * 8 + (P(),) + (P("leaf", None),) * 3,
        out_specs=(tokens,) * 6 + (P(("leaf", "seq"), None),),
        check_vma=False,
    )
```
